32 devices in a mesh: gx: 4 (over y, core), gy: 8 (over z, x).
Axes of the slice: x: 2, y: 2, z: 4, core: 2. Of those that a mesh axis runs over, the one named last changes fastest.
Arguments:
- depth: float32 [16, 64, 1024], P(None, 'gx', 'gy'), may hold values from 0.5 to 2
- momentum: float32 [3, 16, 64, 1024], P(None, None, 'gx', 'gy'), may hold values from -2.5 to 2.5
- tracer: float32 [16, 64, 1024], P(None, 'gx', 'gy'), may hold values from -6 to 6
- cell_wet: int32 [64, 1024], P('gx', 'gy'), may hold values 0 or 1
- tile_wet: int32 [1, 8], replicated, may hold values 0 or 1
Outputs:
- new_depth: float32 [16, 64, 1024], P(None, 'gx', 'gy')
- new_momentum: float32 [3, 16, 64, 1024], P(None, None, 'gx', 'gy')
- new_tracer: float32 [16, 64, 1024], P(None, 'gx', 'gy')
The draws below stay inside these ranges and needn't reach their ends.
All inputs are finite; a program needn't handle non-finite values. No bound on the sum of `cell_wet` on one device may be relied on, other than what follows from the above.
Results may differ from the reference program's by a relative error of at most 0.0003.
Values sent between devices are 32-bit elements; how exact they have to be, the bound alone decides.
A program may use at most 64 MiB of HBM per device.

```python
import jax
import jax.numpy as jnp
from jax import lax

L = 16
ITERS = 3
TILE = 128
NX = 64
NY = 1024
NXT = 1
NYT = 8


def touch_ends(drawn, own_key, smallest, largest):
    longest = drawn.shape.index(max(drawn.shape))
    spots = []
    for shift in (0, 1):
        where = [jax.random.randint(jax.random.fold_in(own_key, axis), (), 0, length) for axis, length in enumerate(drawn.shape)]
        where[longest] = (where[longest] + shift) % drawn.shape[longest]
        spots.append(tuple(where))
    return drawn.at[spots[0]].set(smallest).at[spots[1]].set(largest)


def block_scale(rng, dims, cuts, low, high):
    gain, own = 1.0, jax.random.fold_in(rng, 6)
    for position, parts in cuts:
        steps = jnp.exp(jax.random.uniform(jax.random.fold_in(own, position), (parts,), jnp.float32, low / len(cuts), high / len(cuts)))
        gain = gain * jnp.repeat(steps, dims[position] // parts).reshape([-1 if axis == position else 1 for axis in range(len(dims))])
    return gain


def normal_values(key, extent, width, limit, shards=(), dtype=jnp.bfloat16):
    drawn = jax.random.normal(key, extent, jnp.float32) * width
    if len(shards) > 0:
        drawn = block_scale(key, extent, shards, -0.22, 0.18) * drawn
    return jnp.clip(drawn, min=-limit, max=limit).astype(dtype)


def setup_inputs(seed: int = 0) -> dict:
    seeds = jax.random.split(jax.random.key(seed), 6)
    depth = jnp.clip(0.5 + 1.5 * jax.random.uniform(seeds[0], (L, NX, NY), jnp.float32) ** block_scale(seeds[0], (L, NX, NY), ((1, 4), (2, 8)), -0.2, 0.2), 0.5, 2.0)
    momentum = normal_values(seeds[1], (3, L, NX, NY), 0.3, 2.5, ((2, 4), (3, 8)), jnp.float32)
    tracer = normal_values(seeds[2], (L, NX, NY), 1.0, 6.0, ((1, 4), (2, 8)), jnp.float32)
    cell_wet = touch_ends((jax.random.randint(seeds[3], (NX, NY), 0, 10) < 9).astype(jnp.int32), jax.random.fold_in(seeds[3], 1), 0, 1)
    tile_wet = touch_ends((jax.random.randint(seeds[4], (NXT, NYT), 0, 4) < 3).astype(jnp.int32), jax.random.fold_in(seeds[4], 1), 0, 1)
    return dict(depth=depth, momentum=momentum, tracer=tracer, cell_wet=cell_wet, tile_wet=tile_wet)


gravity = 9.81
time_step = 0.025

def minmod(first_slope, second_slope):
    return 0.5 * (jnp.sign(first_slope) + jnp.sign(second_slope)) * jnp.minimum(jnp.abs(first_slope), jnp.abs(second_slope))

def riemann_flux(left_state, right_state, normal):
    unit_shape = (5,) + (1,) * (left_state.ndim - 1)
    normal_unit = (jnp.arange(5) == normal).astype(jnp.float32).reshape(unit_shape)
    depth_left = left_state[0]
    depth_right = right_state[0]
    speed_left = left_state[normal] / depth_left
    speed_right = right_state[normal] / depth_right
    wave_left = jnp.sqrt(gravity * depth_left)
    wave_right = jnp.sqrt(gravity * depth_right)
    flux_left = left_state * speed_left + normal_unit * (0.5 * gravity * depth_left * depth_left)
    flux_right = right_state * speed_right + normal_unit * (0.5 * gravity * depth_right * depth_right)
    lower_speed = jnp.minimum(jnp.minimum(speed_left - wave_left, speed_right - wave_right), 0.0)
    upper_speed = jnp.maximum(jnp.maximum(speed_left + wave_left, speed_right + wave_right), 0.0)
    return (upper_speed * flux_left - lower_speed * flux_right + lower_speed * upper_speed * (right_state - left_state)) / (upper_speed - lower_speed)

def face_flux(fields, wetness, direction, normal):
    face_count = fields.shape[direction] - 3

    def window(values, offset):
        return lax.slice_in_dim(values, offset, offset + face_count, axis=values.ndim + direction)
    behind = window(fields, 0)
    centre = window(fields, 1)
    onward = window(fields, 2)
    beyond = window(fields, 3)
    left_state = centre + 0.5 * minmod(centre - behind, onward - centre)
    right_state = onward - 0.5 * minmod(onward - centre, beyond - onward)
    return riemann_flux(left_state, right_state, normal) * (window(wetness, 1) * window(wetness, 2))

def section_rate(fields, wetness):
    layer_depth = fields[0] * wetness + (1.0 - wetness)
    usable = jnp.concatenate([layer_depth[None], fields[1:]], 0)
    east_flux = face_flux(usable[..., 2:-2], wetness[:, 2:-2], -2, 1)
    north_flux = face_flux(usable[..., 2:-2, :], wetness[2:-2, :], -1, 2)
    return -time_step * (east_flux[..., 1:, :] - east_flux[..., :-1, :] + (north_flux[..., 1:] - north_flux[..., :-1]))

def advance(fields, wetness_wide):

    def widen(values):
        return jnp.pad(values, ((0, 0), (2, 2), (2, 2)))
    section_one = fields + section_rate(widen(fields), wetness_wide)
    section_two = 0.75 * fields + 0.25 * (section_one + section_rate(widen(section_one), wetness_wide))
    return fields / 3.0 + 2.0 / 3.0 * (section_two + section_rate(widen(section_two), wetness_wide))

def coefficients(columns, vertical_momentum, wetness_cycle):
    depth_wide = columns[0]
    inside = wetness_cycle[1:-1, 1:-1]
    layer_depth = depth_wide[:, 1:-1, 1:-1]
    east_west = 0.5 * (depth_wide[:, :-1, 1:-1] + depth_wide[:, 1:, 1:-1]) * (wetness_cycle[:-1, 1:-1] * wetness_cycle[1:, 1:-1])
    north_south = 0.5 * (depth_wide[:, 1:-1, :-1] + depth_wide[:, 1:-1, 1:]) * (wetness_cycle[1:-1, :-1] * wetness_cycle[1:-1, 1:])
    between = 2.0 * inside / (layer_depth[:-1] + layer_depth[1:])
    surface = 2.0 * inside / layer_depth[-1:]
    nothing = jnp.zeros_like(surface)
    downward = jnp.concatenate([nothing, between], 0)
    upward = jnp.concatenate([between, surface], 0)
    diagonal = 0.5 * layer_depth + east_west[:, :-1] + east_west[:, 1:] + north_south[:, :, :-1] + north_south[:, :, 1:] + downward + upward
    lower_momentum = jnp.concatenate([jnp.zeros_like(vertical_momentum[:1]), vertical_momentum[:-1]], 0)
    divergence = 0.5 * (columns[1][:, 2:, 1:-1] - columns[1][:, :-2, 1:-1]) + 0.5 * (columns[2][:, 1:-1, 2:] - columns[2][:, 1:-1, :-2]) + (vertical_momentum - lower_momentum)
    forcing = -divergence * inside
    return (east_west, north_south, downward, upward, diagonal, forcing)

def apply_operator(pressure_wide, system):
    east_west, north_south, downward, upward, diagonal, forcing = system
    centre = pressure_wide[:, 1:-1, 1:-1]
    nothing = jnp.zeros_like(centre[:1])
    neighbour = east_west[:, :-1] * pressure_wide[:, :-2, 1:-1] + east_west[:, 1:] * pressure_wide[:, 2:, 1:-1]
    neighbour = neighbour + north_south[:, :, :-1] * pressure_wide[:, 1:-1, :-2] + north_south[:, :, 1:] * pressure_wide[:, 1:-1, 2:]
    vertical = downward * jnp.concatenate([nothing, centre[:-1]], 0) + upward * jnp.concatenate([centre[1:], nothing], 0)
    return diagonal * centre - neighbour - vertical

def correct(pressure_wide, system, momentum):
    east_west, north_south, downward, upward, diagonal, forcing = system
    centre = pressure_wide[:, 1:-1, 1:-1]
    nothing = jnp.zeros_like(centre[:1])
    push_east = 0.5 * (east_west[:, 1:] * (pressure_wide[:, 2:, 1:-1] - centre) + east_west[:, :-1] * (centre - pressure_wide[:, :-2, 1:-1]))
    push_north = 0.5 * (north_south[:, :, 1:] * (pressure_wide[:, 1:-1, 2:] - centre) + north_south[:, :, :-1] * (centre - pressure_wide[:, 1:-1, :-2]))
    push_upward = upward * (jnp.concatenate([centre[1:], nothing], 0) - centre)
    return momentum - jnp.stack([push_east, push_north, push_upward])

def reference(depth, momentum, tracer, cell_wet, tile_wet):
    tiles = jnp.repeat(jnp.repeat(tile_wet, TILE, axis=0), TILE, axis=1)[:NX, :NY]
    wetness = (cell_wet * tiles).astype(jnp.float32)
    wetness_wide = jnp.pad(wetness, 2)
    fields = jnp.concatenate([depth[None], momentum, tracer[None]], 0)
    layered = lax.map(lambda layer_fields: advance(layer_fields, wetness_wide), jnp.moveaxis(fields, 1, 0))
    result = jnp.moveaxis(layered, 0, 1)
    columns = jnp.pad(result[:3], ((0, 0), (0, 0), (1, 1), (1, 1)))
    system = coefficients(columns, result[3], wetness_wide[1:-1, 1:-1])
    diagonal = system[4]
    forcing = system[5]
    pressure = jnp.zeros_like(forcing)
    residual = forcing
    scaled = residual / diagonal
    direction = scaled
    energy = jnp.sum(residual * scaled)
    for sweep in range(ITERS):
        applied = apply_operator(jnp.pad(direction, ((0, 0), (1, 1), (1, 1))), system)
        step_size = energy / jnp.sum(direction * applied)
        pressure = pressure + step_size * direction
        residual = residual - step_size * applied
        if sweep + 1 < ITERS:
            scaled = residual / diagonal
            fresh = jnp.sum(residual * scaled)
            direction = scaled + fresh / energy * direction
            energy = fresh
    pressure_wide = jnp.pad(pressure, ((0, 0), (1, 1), (1, 1)))
    new_momentum = correct(pressure_wide, system, result[1:4])
    return (result[0], new_momentum, result[4])
```

```python
import functools

import jax
import jax.numpy as jnp
from jax import lax
from jax.experimental import pallas as pl
from jax.experimental.pallas import tpu as pltpu
from jax.sharding import PartitionSpec as P

ITERS = 3
TILE = 128
REACH = 2 * 3 + 1 + ITERS
SEG = 11

gravity = 9.81
time_step = 0.025
MESH = pl.DeviceIdType.MESH


def minmod(a, b):
    return jnp.maximum(jnp.minimum(a, b), 0.0) + jnp.minimum(jnp.maximum(a, b), 0.0)


def hll(left, right, weight, normal):
    hl, hr = left[0], right[0]
    ul, ur = left[normal] / hl, right[normal] / hr
    al, ar = jnp.sqrt(gravity * hl), jnp.sqrt(gravity * hr)
    lower = jnp.minimum(jnp.minimum(ul - al, ur - ar), 0.0)
    upper = jnp.maximum(jnp.maximum(ul + al, ur + ar), 0.0)
    scale = weight / (upper - lower)
    low, high = lower * scale, upper * scale
    take_left = high * (ul - lower)
    take_right = low * (upper - ur)
    flux = [take_left * l + take_right * r for l, r in zip(left, right)]
    flux[normal] = flux[normal] + (0.5 * gravity) * (high * hl * hl - low * hr * hr)
    return flux


def lane_next(x):
    return pltpu.roll(x, x.shape[-1] - 1, 1)


def lane_prev(x):
    return pltpu.roll(x, 1, 1)


def kernel(
    nx, ny, rows, cols, layers,
    tile_ref, depth_ref, mom_ref, tracer_ref, wet_ref,
    depth_out, mom_out, tracer_out,
    fa, fb, fc, wet, pack_l, pack_r, halo_l, halo_r,
    ce, cn, up, inv, z0, z1, z2, part, gather_x, gather_y,
    send_row, recv_row, send_wet, recv_wet, send_col, recv_col,
    send_cor, recv_cor, send_gx, recv_gx, send_gy, recv_gy,
):
    R = REACH
    high_rows = rows + 2 * R
    width = 2 * cols
    half = layers // 2
    gx, gy = lax.axis_index("gx"), lax.axis_index("gy")

    fa[...] = jnp.zeros_like(fa)
    wet[...] = jnp.zeros_like(wet)
    halo_l[...] = jnp.zeros_like(halo_l)
    halo_r[...] = jnp.zeros_like(halo_r)

    barrier = pltpu.get_barrier_semaphore()
    has = {-1: gx > 0, 1: gx < nx - 1}
    side = {-1: gy > 0, 1: gy < ny - 1}
    for o in range(1, nx):
        pl.semaphore_signal(barrier, inc=1, device_id=(lax.rem(gx + o, nx), gy), device_id_type=MESH)
    for o in range(1, ny):
        pl.semaphore_signal(barrier, inc=1, device_id=(gx, lax.rem(gy + o, ny)), device_id_type=MESH)
    for dx in (-1, 1):
        for dy in (-1, 1):
            @pl.when(jnp.logical_and(has[dx], side[dy]))
            def _(dx=dx, dy=dy):
                pl.semaphore_signal(barrier, inc=1, device_id=(gx + dx, gy + dy), device_id_type=MESH)

    tile = tile_ref[(gx * rows) // TILE, (gy * cols) // TILE].astype(jnp.float32)
    for r in range(rows):
        wet[R + r, :, :cols] = wet_ref[r : r + 1, :].astype(jnp.float32) * tile

    def load_row(r, carry):
        at = pl.ds(r, layers, stride=rows)
        fa[0, R + r, :, :cols] = depth_ref[at, :]
        for n in range(3):
            fa[1 + n, R + r, :, :cols] = mom_ref[n, at, :]
        fa[4, R + r, :, :cols] = tracer_ref[at, :]
        return carry

    lax.fori_loop(0, rows, load_row, 0)

    lane = lax.broadcasted_iota(jnp.int32, (half, cols), 1)

    def pack_row(r, carry):
        left = jnp.zeros((half, cols), jnp.float32)
        right = left
        for s in range(11):
            if s < 10:
                x = fa[s % 5, R + r, (s // 5) * half : (s // 5 + 1) * half, :cols]
            else:
                x = jnp.broadcast_to(wet[R + r, :, :cols], (half, cols))
            mask = jnp.logical_and(lane >= SEG * s, lane < SEG * s + R)
            left = jnp.where(mask, pltpu.roll(x, SEG * s, 1) if s else x, left)
            right = jnp.where(mask, pltpu.roll(x, (SEG * s + R) % cols, 1), right)
        pack_l[r] = left
        pack_r[r] = right
        return carry

    lax.fori_loop(0, rows, pack_row, 0)

    as_int = lambda flag: flag.astype(jnp.int32)
    corners = (as_int(has[-1]) + as_int(has[1])) * (as_int(side[-1]) + as_int(side[1]))
    pl.semaphore_wait(barrier, nx - 1 + ny - 1 + corners)

    copies = []
    mine = {-1: R, 1: rows}
    theirs = {-1: R + rows, 1: 0}
    pack = {-1: pack_l, 1: pack_r}
    halo = {-1: halo_r, 1: halo_l}
    for i, dx in enumerate((-1, 1)):
        for src, send, recv in ((fa, send_row, recv_row), (wet, send_wet, recv_wet)):
            if src is fa:
                a = fa.at[:, pl.ds(mine[dx], R), :, pl.ds(0, cols)]
                b = fa.at[:, pl.ds(theirs[dx], R), :, pl.ds(0, cols)]
            else:
                a = wet.at[pl.ds(mine[dx], R), :, pl.ds(0, cols)]
                b = wet.at[pl.ds(theirs[dx], R), :, pl.ds(0, cols)]
            send_to = pltpu.make_async_remote_copy(
                src_ref=a, dst_ref=b, send_sem=send.at[i], recv_sem=recv.at[i],
                device_id=(gx + dx, gy), device_id_type=MESH)
            come = pltpu.make_async_remote_copy(
                src_ref=a, dst_ref=b, send_sem=send.at[i], recv_sem=recv.at[1 - i],
                device_id=(gx + dx, gy), device_id_type=MESH)
            copies.append((has[dx], send_to, come))
    for j, dy in enumerate((-1, 1)):
        args = dict(src_ref=pack[dy], dst_ref=halo[dy].at[pl.ds(R, rows)], send_sem=send_col.at[j],
                    device_id=(gx, gy + dy), device_id_type=MESH)
        copies.append((side[dy],
                       pltpu.make_async_remote_copy(recv_sem=recv_col.at[j], **args),
                       pltpu.make_async_remote_copy(recv_sem=recv_col.at[1 - j], **args)))
        for i, dx in enumerate((-1, 1)):
            args = dict(src_ref=pack[dy].at[pl.ds(mine[dx] - R, R)],
                        dst_ref=halo[dy].at[pl.ds(theirs[dx], R)],
                        send_sem=send_cor.at[i, j],
                        device_id=(gx + dx, gy + dy), device_id_type=MESH)
            copies.append((jnp.logical_and(has[dx], side[dy]),
                           pltpu.make_async_remote_copy(recv_sem=recv_cor.at[i, j], **args),
                           pltpu.make_async_remote_copy(recv_sem=recv_cor.at[1 - i, 1 - j], **args)))
    for cond, go, come in copies:
        @pl.when(cond)
        def _(go=go):
            go.start()
    for cond, go, come in copies:
        @pl.when(cond)
        def _(go=go, come=come):
            go.wait_send()
            come.wait_recv()

    def unpack_row(r, carry):
        fr, fl = halo_r[r], halo_l[r]
        for s in range(11):
            a = pltpu.roll(fr, cols - SEG * s, 1) if s else fr
            b = pltpu.roll(fl, cols - R - SEG * s if SEG * s + R < cols else 2 * cols - R - SEG * s, 1)
            x = jnp.where(lane < R, a, jnp.where(lane >= cols - R, b, 0.0))
            if s < 10:
                fa[s % 5, r, (s // 5) * half : (s // 5 + 1) * half, cols:] = x
            else:
                wet[r, :, cols:] = x[:1]
        return carry

    lax.fori_loop(0, high_rows, unpack_row, 0)

    def transport(src, dst, lo, hi, keep):
        for part_of in range(2):
            cut = slice(part_of * half, (part_of + 1) * half)

            def usable(r):
                w = wet[r]
                u = [src[f, r, cut, :] for f in range(5)]
                u[0] = u[0] * w + (1.0 - w)
                return u

            def sides(u, before, after):
                s = [0.5 * minmod(b, a) for b, a in zip(before, after)]
                return [x - y for x, y in zip(u, s)], [x + y for x, y in zip(u, s)]

            def row_face(i, left):
                here, mid, far = usable(i), usable(i + 1), usable(i + 2)
                right, following = sides(
                    mid, [m - h for m, h in zip(mid, here)], [f - m for f, m in zip(far, mid)])
                return hll(left, right, wet[i] * wet[i + 1], 1), following

            def step(i, carry):
                flux_low, left = carry
                flux_high, following = row_face(i, left)
                u = usable(i)
                d = [lane_next(x) - x for x in u]
                right, left_c = sides(u, [lane_prev(x) for x in d], d)
                w = wet[i]
                across = hll(left_c, [lane_next(x) for x in right], w * lane_next(jnp.broadcast_to(w, (half, width))), 2)
                for f in range(5):
                    rate = -time_step * (flux_high[f] - flux_low[f] + (across[f] - lane_prev(across[f])))
                    old = src[f, i, cut, :]
                    if keep is None:
                        new = old + rate
                    elif keep == 0.75:
                        new = 0.75 * fa[f, i, cut, :] + 0.25 * (old + rate)
                    else:
                        new = fa[f, i, cut, :] * (1.0 / 3.0) + (2.0 / 3.0) * (old + rate)
                    dst[f, i, cut, :] = new
                return flux_high, following

            a, b, c = usable(lo - 2), usable(lo - 1), usable(lo)
            _, left = sides(b, [y - x for x, y in zip(a, b)], [y - x for x, y in zip(b, c)])
            flux, left = row_face(lo - 1, left)
            lax.fori_loop(lo, hi, step, (flux, left))

    transport(fa, fb, 2, high_rows - 2, None)
    transport(fb, fc, 4, high_rows - 4, 0.75)
    transport(fc, fb, 6, high_rows - 6, 1.0 / 3.0)

    layer_id = lax.broadcasted_iota(jnp.int32, (layers, width), 0)
    top = layer_id == layers - 1

    def above(x):
        return pltpu.roll(x, layers - 1, 0)

    def below(x):
        return pltpu.roll(x, 1, 0)

    def prepare(r, low):
        h, w = fb[0, r], wet[r]
        high = 0.5 * (h + fb[0, r + 1]) * (w * wet[r + 1])
        across = 0.5 * (h + lane_next(h)) * (w * lane_next(jnp.broadcast_to(w, (layers, width))))
        total = jnp.where(top, h, h + above(h))
        upward = jnp.where(jnp.broadcast_to(w, total.shape) > 0.0, 2.0 / total, 0.0)
        inner = jnp.where(top, 0.0, upward)
        diagonal = 0.5 * h + low + high + lane_prev(across) + across + below(inner) + upward
        v = fb[3, r]
        y = fb[2, r]
        div = (
            0.5 * (fb[1, r + 1] - fb[1, r - 1])
            + 0.5 * (lane_next(y) - lane_prev(y))
            + (v - jnp.where(layer_id == 0, 0.0, below(v)))
        )
        force = -div * w
        inverse = jnp.where(diagonal == 0.0, 0.0, 1.0 / diagonal)
        ce[r] = high
        cn[r] = across
        up[r] = upward
        inv[r] = inverse
        z = force * inverse
        z0[r] = z
        return high, force, z

    def fold(x):
        return x[:half, :cols] + x[half:, :cols]

    first = REACH - ITERS
    ce[first - 1] = 0.5 * (fb[0, first - 1] + fb[0, first]) * (wet[first - 1] * wet[first])

    def prep_outer(r, low):
        return prepare(r, low)[0]

    def prep_inner(r, carry):
        low, acc = carry
        high, force, z = prepare(r, low)
        return high, acc + fold(force * z)

    zero = jnp.zeros((half, cols), jnp.float32)
    low = lax.fori_loop(first, R, prep_outer, ce[first - 1])
    low, m0 = lax.fori_loop(R, R + rows, prep_inner, (low, zero))
    lax.fori_loop(R + rows, R + rows + ITERS, prep_outer, low)

    def spread(z, r):
        x = z[r]
        c = cn[r]
        u = jnp.where(top, 0.0, up[r])
        return (
            ce[r - 1] * z[r - 1] + ce[r] * z[r + 1]
            + c * lane_next(x) + lane_prev(c * x)
            + u * above(x) + below(u * x)
        )

    def advance(z, target, reach):
        def outer(r, carry):
            target[r] = spread(z, r) * inv[r]
            return carry

        def inner(r, carry):
            odd, even = carry
            n = spread(z, r)
            y = n * inv[r]
            target[r] = y
            return odd + fold(z[r] * n), even + fold(y * n)

        lax.fori_loop(R - reach, R, outer, 0)
        sums = lax.fori_loop(R, R + rows, inner, (zero, zero))
        lax.fori_loop(R + rows, R + rows + reach, outer, 0)
        return sums

    m1, m2 = advance(z0, z1, 2)
    m3, m4 = advance(z1, z2, 1)
    m5 = lax.fori_loop(R, R + rows, lambda r, acc: acc + fold(z2[r] * spread(z2, r)), zero)

    part[0] = jnp.zeros((8, cols), jnp.float32)
    for k, m in enumerate((m0, m1, m2, m3, m4, m5)):
        part[0, k : k + 1, :] = jnp.sum(m, axis=0, keepdims=True)

    def everyone(count, slot, gather, send, recv, place):
        moves = [
            pltpu.make_async_remote_copy(
                src_ref=part.at[slot], dst_ref=gather.at[o - 1], send_sem=send.at[o - 1],
                recv_sem=recv.at[o - 1], device_id=place(o), device_id_type=MESH)
            for o in range(1, count)
        ]
        for move in moves:
            move.start()
        for move in moves:
            move.wait()
        return moves

    everyone(nx, 0, gather_x, send_gx, recv_gx, lambda o: (lax.rem(gx + o, nx), gy))
    total = part[0]
    for o in range(nx - 1):
        total = total + gather_x[o]
    part[1] = total
    everyone(ny, 1, gather_y, send_gy, recv_gy, lambda o: (gx, lax.rem(gy + o, ny)))
    for o in range(ny - 1):
        total = total + gather_y[o]
    sums = jnp.broadcast_to(jnp.sum(total, axis=1, keepdims=True), (8, width))
    m = [sums[k : k + 1, :] for k in range(6)]

    def dots(a, b, table):
        out = None
        for i in range(3):
            for j in range(3):
                if a[i] is not None and b[j] is not None:
                    t = a[i] * b[j] * table[i + j]
                    out = t if out is None else out + t
        return out

    shifted = [m[k] - m[k + 1] for k in range(5)]

    def plus(a, b, f):
        out = []
        for x, y in zip(a, b):
            out.append(x if y is None else (f * y if x is None else x + f * y))
        return out

    def image(d):
        moved = [None, d[0], d[1]]
        return [x if y is None else (None if x is None and y is None else (-y if x is None else x - y)) for x, y in zip(d, moved)]

    one = jnp.ones_like(m[0])
    direction = [one, None, None]
    residual = [one, None, None]
    pressure = [None, None, None]
    energy = m[0]
    for sweep in range(ITERS):
        bottom = dots(direction, direction, shifted)
        size = energy / bottom
        pressure = plus(pressure, direction, size)
        if sweep + 1 < ITERS:
            residual = plus(residual, image(direction), -size)
            fresh = dots(residual, residual, m)
            direction = plus(residual, direction, fresh / energy)
            energy = fresh

    def solve(r, carry):
        z0[r] = pressure[0] * z0[r] + pressure[1] * z1[r] + pressure[2] * z2[r]
        return carry

    lax.fori_loop(R - 1, R + rows + 1, solve, 0)

    def correct(r, carry):
        q, c = z0[r], cn[r]
        east = 0.5 * (ce[r] * (z0[r + 1] - q) + ce[r - 1] * (q - z0[r - 1]))
        slope = c * (lane_next(q) - q)
        north = 0.5 * (slope + lane_prev(slope))
        upward = up[r] * (jnp.where(top, 0.0, above(q)) - q)
        at = pl.ds(r - R, layers, stride=rows)
        depth_out[at, :] = fb[0, r, :, :cols]
        tracer_out[at, :] = fb[4, r, :, :cols]
        for n, push in enumerate((east, north, upward)):
            mom_out[n, at, :] = fb[1 + n, r, :, :cols] - push[:, :cols]
        return carry

    lax.fori_loop(R, R + rows, correct, 0)


def body(nx, ny, depth, momentum, tracer, cell_wet, tile_wet):
    layers, rows, cols = depth.shape
    assert TILE % rows == 0 and TILE % cols == 0 and cols == 128 and rows >= REACH
    f32 = jnp.float32
    tall = rows + 2 * REACH
    wide = 2 * cols
    half = layers // 2
    dma = pltpu.SemaphoreType.DMA
    vmem = pl.BlockSpec(memory_space=pltpu.VMEM)
    flat = jax.ShapeDtypeStruct((layers * rows, cols), f32)
    field = pltpu.VMEM((5, tall, layers, wide), f32)
    layer = pltpu.VMEM((tall, layers, wide), f32)
    packed = pltpu.VMEM((rows, half, cols), f32)
    halo = pltpu.VMEM((tall, half, cols), f32)
    pairs = [dma((2,))] * 6 + [dma((2, 2))] * 2 + [dma((nx - 1,))] * 2 + [dma((ny - 1,))] * 2
    new_depth, new_momentum, new_tracer = pl.pallas_call(
        functools.partial(kernel, nx, ny, rows, cols, layers),
        out_shape=(flat, jax.ShapeDtypeStruct((3, layers * rows, cols), f32), flat),
        in_specs=[pl.BlockSpec(memory_space=pltpu.SMEM)] + [vmem] * 4,
        out_specs=(vmem, vmem, vmem),
        scratch_shapes=[
            field, field, field,
            pltpu.VMEM((tall, 1, wide), f32),
            packed, packed, halo, halo,
            layer, layer, layer, layer, layer, layer, layer,
            pltpu.VMEM((2, 8, cols), f32),
            pltpu.VMEM((nx - 1, 8, cols), f32),
            pltpu.VMEM((ny - 1, 8, cols), f32),
            *pairs,
        ],
        compiler_params=pltpu.CompilerParams(
            collective_id=0, has_side_effects=True, vmem_limit_bytes=40 * 1024 * 1024
        ),
    )(
        tile_wet,
        depth.reshape(layers * rows, cols),
        momentum.reshape(3, layers * rows, cols),
        tracer.reshape(layers * rows, cols),
        cell_wet,
    )
    return (
        new_depth.reshape(depth.shape),
        new_momentum.reshape(momentum.shape),
        new_tracer.reshape(tracer.shape),
    )


def solution(mesh):
    placed = (
        P(None, "gx", "gy"),
        P(None, None, "gx", "gy"),
        P(None, "gx", "gy"),
        P("gx", "gy"),
        P(),
    )
    return jax.shard_map(
        functools.partial(body, mesh.shape["gx"], mesh.shape["gy"]),
        mesh=mesh,
        in_specs=placed,
        out_specs=(P(None, "gx", "gy"), P(None, None, "gx", "gy"), P(None, "gx", "gy")),
        check_vma=False,
    )
```

```python
import functools

import jax
import jax.numpy as jnp
from jax import lax
from jax.experimental import pallas as pl
from jax.experimental.pallas import tpu as pltpu
from jax.sharding import PartitionSpec as P

ITERS = 3
TILE = 128
REACH = 2 * 3 + 1 + ITERS
SEG = 11

gravity = 9.81
time_step = 0.025
MESH = pl.DeviceIdType.MESH


def minmod(a, b):
    return jnp.maximum(jnp.minimum(a, b), 0.0) + jnp.minimum(jnp.maximum(a, b), 0.0)


def hll(left, right, weight, normal):
    hl, hr = left[0], right[0]
    rl, rr = lax.rsqrt(hl), lax.rsqrt(hr)
    ul, ur = left[normal] * (rl * rl), right[normal] * (rr * rr)
    al, ar = gravity**0.5 * (hl * rl), gravity**0.5 * (hr * rr)
    lower = jnp.minimum(jnp.minimum(ul - al, ur - ar), 0.0)
    upper = jnp.maximum(jnp.maximum(ul + al, ur + ar), 0.0)
    scale = weight / (upper - lower)
    low, high = lower * scale, upper * scale
    take_left = high * (ul - lower)
    take_right = low * (upper - ur)
    flux = [take_left * l + take_right * r for l, r in zip(left, right)]
    flux[normal] = flux[normal] + (0.5 * gravity) * (high * hl * hl - low * hr * hr)
    return flux


def lane_next(x):
    return pltpu.roll(x, x.shape[-1] - 1, 1)


def lane_prev(x):
    return pltpu.roll(x, 1, 1)


def kernel(
    nx, ny, rows, cols, layers,
    tile_ref, depth_ref, mom_ref, tracer_ref, wet_ref,
    depth_out, mom_out, tracer_out,
    fa, fb, fc, wet, pack_l, pack_r, halo_l, halo_r,
    ce, cn, up, inv, z0, z1, z2, part, gather_x, gather_y,
    send_row, recv_row, send_wet, recv_wet, send_col, recv_col,
    send_cor, recv_cor, send_gx, recv_gx, send_gy, recv_gy,
):
    R = REACH
    high_rows = rows + 2 * R
    width = 2 * cols
    half = layers // 2
    gx, gy = lax.axis_index("gx"), lax.axis_index("gy")

    fa[...] = jnp.zeros_like(fa)
    wet[...] = jnp.zeros_like(wet)
    halo_l[...] = jnp.zeros_like(halo_l)
    halo_r[...] = jnp.zeros_like(halo_r)

    barrier = pltpu.get_barrier_semaphore()
    has = {-1: gx > 0, 1: gx < nx - 1}
    side = {-1: gy > 0, 1: gy < ny - 1}
    for o in range(1, nx):
        pl.semaphore_signal(barrier, inc=1, device_id=(lax.rem(gx + o, nx), gy), device_id_type=MESH)
    for o in range(1, ny):
        pl.semaphore_signal(barrier, inc=1, device_id=(gx, lax.rem(gy + o, ny)), device_id_type=MESH)
    for dx in (-1, 1):
        for dy in (-1, 1):
            @pl.when(jnp.logical_and(has[dx], side[dy]))
            def _(dx=dx, dy=dy):
                pl.semaphore_signal(barrier, inc=1, device_id=(gx + dx, gy + dy), device_id_type=MESH)

    tile = tile_ref[(gx * rows) // TILE, (gy * cols) // TILE].astype(jnp.float32)
    for r in range(rows):
        wet[R + r, :, :cols] = wet_ref[r : r + 1, :].astype(jnp.float32) * tile

    def load_row(r, carry):
        at = pl.ds(r, layers, stride=rows)
        fa[0, R + r, :, :cols] = depth_ref[at, :]
        for n in range(3):
            fa[1 + n, R + r, :, :cols] = mom_ref[n, at, :]
        fa[4, R + r, :, :cols] = tracer_ref[at, :]
        return carry

    lax.fori_loop(0, rows, load_row, 0, unroll=4)

    lane = lax.broadcasted_iota(jnp.int32, (half, cols), 1)

    def pack_row(r, carry):
        left = jnp.zeros((half, cols), jnp.float32)
        right = left
        for s in range(11):
            if s < 10:
                x = fa[s % 5, R + r, (s // 5) * half : (s // 5 + 1) * half, :cols]
            else:
                x = jnp.broadcast_to(wet[R + r, :, :cols], (half, cols))
            mask = jnp.logical_and(lane >= SEG * s, lane < SEG * s + R)
            left = jnp.where(mask, pltpu.roll(x, SEG * s, 1) if s else x, left)
            right = jnp.where(mask, pltpu.roll(x, (SEG * s + R) % cols, 1), right)
        pack_l[r] = left
        pack_r[r] = right
        return carry

    lax.fori_loop(0, rows, pack_row, 0, unroll=4)

    as_int = lambda flag: flag.astype(jnp.int32)
    corners = (as_int(has[-1]) + as_int(has[1])) * (as_int(side[-1]) + as_int(side[1]))
    pl.semaphore_wait(barrier, nx - 1 + ny - 1 + corners)

    copies = []
    mine = {-1: R, 1: rows}
    theirs = {-1: R + rows, 1: 0}
    pack = {-1: pack_l, 1: pack_r}
    halo = {-1: halo_r, 1: halo_l}
    for i, dx in enumerate((-1, 1)):
        for src, send, recv in ((fa, send_row, recv_row), (wet, send_wet, recv_wet)):
            if src is fa:
                a = fa.at[:, pl.ds(mine[dx], R), :, pl.ds(0, cols)]
                b = fa.at[:, pl.ds(theirs[dx], R), :, pl.ds(0, cols)]
            else:
                a = wet.at[pl.ds(mine[dx], R), :, pl.ds(0, cols)]
                b = wet.at[pl.ds(theirs[dx], R), :, pl.ds(0, cols)]
            send_to = pltpu.make_async_remote_copy(
                src_ref=a, dst_ref=b, send_sem=send.at[i], recv_sem=recv.at[i],
                device_id=(gx + dx, gy), device_id_type=MESH)
            come = pltpu.make_async_remote_copy(
                src_ref=a, dst_ref=b, send_sem=send.at[i], recv_sem=recv.at[1 - i],
                device_id=(gx + dx, gy), device_id_type=MESH)
            copies.append((has[dx], send_to, come))
    for j, dy in enumerate((-1, 1)):
        args = dict(src_ref=pack[dy], dst_ref=halo[dy].at[pl.ds(R, rows)], send_sem=send_col.at[j],
                    device_id=(gx, gy + dy), device_id_type=MESH)
        copies.append((side[dy],
                       pltpu.make_async_remote_copy(recv_sem=recv_col.at[j], **args),
                       pltpu.make_async_remote_copy(recv_sem=recv_col.at[1 - j], **args)))
        for i, dx in enumerate((-1, 1)):
            args = dict(src_ref=pack[dy].at[pl.ds(mine[dx] - R, R)],
                        dst_ref=halo[dy].at[pl.ds(theirs[dx], R)],
                        send_sem=send_cor.at[i, j],
                        device_id=(gx + dx, gy + dy), device_id_type=MESH)
            copies.append((jnp.logical_and(has[dx], side[dy]),
                           pltpu.make_async_remote_copy(recv_sem=recv_cor.at[i, j], **args),
                           pltpu.make_async_remote_copy(recv_sem=recv_cor.at[1 - i, 1 - j], **args)))
    for cond, go, come in copies:
        @pl.when(cond)
        def _(go=go):
            go.start()
    for cond, go, come in copies:
        @pl.when(cond)
        def _(go=go, come=come):
            go.wait_send()
            come.wait_recv()

    def unpack_row(r, carry):
        fr, fl = halo_r[r], halo_l[r]
        for s in range(11):
            a = pltpu.roll(fr, cols - SEG * s, 1) if s else fr
            b = pltpu.roll(fl, cols - R - SEG * s if SEG * s + R < cols else 2 * cols - R - SEG * s, 1)
            x = jnp.where(lane < R, a, jnp.where(lane >= cols - R, b, 0.0))
            if s < 10:
                fa[s % 5, r, (s // 5) * half : (s // 5 + 1) * half, cols:] = x
            else:
                wet[r, :, cols:] = x[:1]
        return carry

    lax.fori_loop(0, high_rows, unpack_row, 0, unroll=4)

    def transport(src, dst, lo, hi, keep):
        for part_of in range(2):
            cut = slice(part_of * half, (part_of + 1) * half)

            def usable(r):
                w = wet[r]
                u = [src[f, r, cut, :] for f in range(5)]
                u[0] = u[0] * w + (1.0 - w)
                return u

            def sides(u, before, after):
                s = [0.5 * minmod(b, a) for b, a in zip(before, after)]
                return [x - y for x, y in zip(u, s)], [x + y for x, y in zip(u, s)]

            def row_face(i, left):
                here, mid, far = usable(i), usable(i + 1), usable(i + 2)
                right, following = sides(
                    mid, [m - h for m, h in zip(mid, here)], [f - m for f, m in zip(far, mid)])
                return hll(left, right, wet[i] * wet[i + 1], 1), following

            def step(i, carry):
                flux_low, left = carry
                flux_high, following = row_face(i, left)
                u = usable(i)
                d = [lane_next(x) - x for x in u]
                right, left_c = sides(u, [lane_prev(x) for x in d], d)
                w = wet[i]
                across = hll(left_c, [lane_next(x) for x in right], w * lane_next(jnp.broadcast_to(w, (half, width))), 2)
                for f in range(5):
                    rate = -time_step * (flux_high[f] - flux_low[f] + (across[f] - lane_prev(across[f])))
                    old = src[f, i, cut, :]
                    if keep is None:
                        new = old + rate
                    elif keep == 0.75:
                        new = 0.75 * fa[f, i, cut, :] + 0.25 * (old + rate)
                    else:
                        new = fa[f, i, cut, :] * (1.0 / 3.0) + (2.0 / 3.0) * (old + rate)
                    dst[f, i, cut, :] = new
                return flux_high, following

            a, b, c = usable(lo - 2), usable(lo - 1), usable(lo)
            _, left = sides(b, [y - x for x, y in zip(a, b)], [y - x for x, y in zip(b, c)])
            flux, left = row_face(lo - 1, left)
            lax.fori_loop(lo, hi, step, (flux, left), unroll=4)

    transport(fa, fb, 2, high_rows - 2, None)
    transport(fb, fc, 4, high_rows - 4, 0.75)
    transport(fc, fb, 6, high_rows - 6, 1.0 / 3.0)

    layer_id = lax.broadcasted_iota(jnp.int32, (layers, width), 0)
    top = layer_id == layers - 1

    def above(x):
        return pltpu.roll(x, layers - 1, 0)

    def below(x):
        return pltpu.roll(x, 1, 0)

    def prepare(r, low):
        h, w = fb[0, r], wet[r]
        high = 0.5 * (h + fb[0, r + 1]) * (w * wet[r + 1])
        across = 0.5 * (h + lane_next(h)) * (w * lane_next(jnp.broadcast_to(w, (layers, width))))
        total = jnp.where(top, h, h + above(h))
        upward = jnp.where(jnp.broadcast_to(w, total.shape) > 0.0, 2.0 / total, 0.0)
        inner = jnp.where(top, 0.0, upward)
        diagonal = 0.5 * h + low + high + lane_prev(across) + across + below(inner) + upward
        v = fb[3, r]
        y = fb[2, r]
        div = (
            0.5 * (fb[1, r + 1] - fb[1, r - 1])
            + 0.5 * (lane_next(y) - lane_prev(y))
            + (v - jnp.where(layer_id == 0, 0.0, below(v)))
        )
        force = -div * w
        inverse = jnp.where(diagonal == 0.0, 0.0, 1.0 / diagonal)
        ce[r] = high
        cn[r] = across
        up[r] = upward
        inv[r] = inverse
        z = force * inverse
        z0[r] = z
        return high, force, z

    def fold(x):
        return x[:half, :cols] + x[half:, :cols]

    first = REACH - ITERS
    ce[first - 1] = 0.5 * (fb[0, first - 1] + fb[0, first]) * (wet[first - 1] * wet[first])

    def prep_outer(r, low):
        return prepare(r, low)[0]

    def prep_inner(r, carry):
        low, acc = carry
        high, force, z = prepare(r, low)
        return high, acc + fold(force * z)

    zero = jnp.zeros((half, cols), jnp.float32)
    low = lax.fori_loop(first, R, prep_outer, ce[first - 1])
    low, m0 = lax.fori_loop(R, R + rows, prep_inner, (low, zero), unroll=4)
    lax.fori_loop(R + rows, R + rows + ITERS, prep_outer, low)

    def spread(z, r):
        x = z[r]
        c = cn[r]
        u = jnp.where(top, 0.0, up[r])
        return (
            ce[r - 1] * z[r - 1] + ce[r] * z[r + 1]
            + c * lane_next(x) + lane_prev(c * x)
            + u * above(x) + below(u * x)
        )

    def advance(z, target, reach):
        def outer(r, carry):
            target[r] = spread(z, r) * inv[r]
            return carry

        def inner(r, carry):
            odd, even = carry
            n = spread(z, r)
            y = n * inv[r]
            target[r] = y
            return odd + fold(z[r] * n), even + fold(y * n)

        lax.fori_loop(R - reach, R, outer, 0)
        sums = lax.fori_loop(R, R + rows, inner, (zero, zero), unroll=4)
        lax.fori_loop(R + rows, R + rows + reach, outer, 0)
        return sums

    m1, m2 = advance(z0, z1, 2)
    m3, m4 = advance(z1, z2, 1)
    m5 = lax.fori_loop(R, R + rows, lambda r, acc: acc + fold(z2[r] * spread(z2, r)), zero, unroll=4)

    part[0] = jnp.zeros((8, cols), jnp.float32)
    for k, m in enumerate((m0, m1, m2, m3, m4, m5)):
        part[0, k : k + 1, :] = jnp.sum(m, axis=0, keepdims=True)

    def everyone(count, slot, gather, send, recv, place):
        moves = [
            pltpu.make_async_remote_copy(
                src_ref=part.at[slot], dst_ref=gather.at[o - 1], send_sem=send.at[o - 1],
                recv_sem=recv.at[o - 1], device_id=place(o), device_id_type=MESH)
            for o in range(1, count)
        ]
        for move in moves:
            move.start()
        for move in moves:
            move.wait()
        return moves

    everyone(nx, 0, gather_x, send_gx, recv_gx, lambda o: (lax.rem(gx + o, nx), gy))
    total = part[0]
    for o in range(nx - 1):
        total = total + gather_x[o]
    part[1] = total
    everyone(ny, 1, gather_y, send_gy, recv_gy, lambda o: (gx, lax.rem(gy + o, ny)))
    for o in range(ny - 1):
        total = total + gather_y[o]
    sums = jnp.broadcast_to(jnp.sum(total, axis=1, keepdims=True), (8, width))
    m = [sums[k : k + 1, :] for k in range(6)]

    def dots(a, b, table):
        out = None
        for i in range(3):
            for j in range(3):
                if a[i] is not None and b[j] is not None:
                    t = a[i] * b[j] * table[i + j]
                    out = t if out is None else out + t
        return out

    shifted = [m[k] - m[k + 1] for k in range(5)]

    def plus(a, b, f):
        out = []
        for x, y in zip(a, b):
            out.append(x if y is None else (f * y if x is None else x + f * y))
        return out

    def image(d):
        moved = [None, d[0], d[1]]
        return [x if y is None else (None if x is None and y is None else (-y if x is None else x - y)) for x, y in zip(d, moved)]

    one = jnp.ones_like(m[0])
    direction = [one, None, None]
    residual = [one, None, None]
    pressure = [None, None, None]
    energy = m[0]
    for sweep in range(ITERS):
        bottom = dots(direction, direction, shifted)
        size = energy / bottom
        pressure = plus(pressure, direction, size)
        if sweep + 1 < ITERS:
            residual = plus(residual, image(direction), -size)
            fresh = dots(residual, residual, m)
            direction = plus(residual, direction, fresh / energy)
            energy = fresh

    def solve(r, carry):
        z0[r] = pressure[0] * z0[r] + pressure[1] * z1[r] + pressure[2] * z2[r]
        return carry

    lax.fori_loop(R - 1, R + rows + 1, solve, 0, unroll=6)

    def correct(r, carry):
        q, c = z0[r], cn[r]
        east = 0.5 * (ce[r] * (z0[r + 1] - q) + ce[r - 1] * (q - z0[r - 1]))
        slope = c * (lane_next(q) - q)
        north = 0.5 * (slope + lane_prev(slope))
        upward = up[r] * (jnp.where(top, 0.0, above(q)) - q)
        at = pl.ds(r - R, layers, stride=rows)
        depth_out[at, :] = fb[0, r, :, :cols]
        tracer_out[at, :] = fb[4, r, :, :cols]
        for n, push in enumerate((east, north, upward)):
            mom_out[n, at, :] = fb[1 + n, r, :, :cols] - push[:, :cols]
        return carry

    lax.fori_loop(R, R + rows, correct, 0, unroll=4)


def body(nx, ny, depth, momentum, tracer, cell_wet, tile_wet):
    layers, rows, cols = depth.shape
    assert TILE % rows == 0 and TILE % cols == 0 and cols == 128 and rows >= REACH
    f32 = jnp.float32
    tall = rows + 2 * REACH
    wide = 2 * cols
    half = layers // 2
    dma = pltpu.SemaphoreType.DMA
    vmem = pl.BlockSpec(memory_space=pltpu.VMEM)
    flat = jax.ShapeDtypeStruct((layers * rows, cols), f32)
    field = pltpu.VMEM((5, tall, layers, wide), f32)
    layer = pltpu.VMEM((tall, layers, wide), f32)
    packed = pltpu.VMEM((rows, half, cols), f32)
    halo = pltpu.VMEM((tall, half, cols), f32)
    pairs = [dma((2,))] * 6 + [dma((2, 2))] * 2 + [dma((nx - 1,))] * 2 + [dma((ny - 1,))] * 2
    new_depth, new_momentum, new_tracer = pl.pallas_call(
        functools.partial(kernel, nx, ny, rows, cols, layers),
        out_shape=(flat, jax.ShapeDtypeStruct((3, layers * rows, cols), f32), flat),
        in_specs=[pl.BlockSpec(memory_space=pltpu.SMEM)] + [vmem] * 4,
        out_specs=(vmem, vmem, vmem),
        scratch_shapes=[
            field, field, field,
            pltpu.VMEM((tall, 1, wide), f32),
            packed, packed, halo, halo,
            layer, layer, layer, layer, layer, layer, layer,
            pltpu.VMEM((2, 8, cols), f32),
            pltpu.VMEM((nx - 1, 8, cols), f32),
            pltpu.VMEM((ny - 1, 8, cols), f32),
            *pairs,
        ],
        compiler_params=pltpu.CompilerParams(
            collective_id=0, has_side_effects=True, vmem_limit_bytes=40 * 1024 * 1024
        ),
    )(
        tile_wet,
        depth.reshape(layers * rows, cols),
        momentum.reshape(3, layers * rows, cols),
        tracer.reshape(layers * rows, cols),
        cell_wet,
    )
    return (
        new_depth.reshape(depth.shape),
        new_momentum.reshape(momentum.shape),
        new_tracer.reshape(tracer.shape),
    )


def solution(mesh):
    placed = (
        P(None, "gx", "gy"),
        P(None, None, "gx", "gy"),
        P(None, "gx", "gy"),
        P("gx", "gy"),
        P(),
    )
    return jax.shard_map(
        functools.partial(body, mesh.shape["gx"], mesh.shape["gy"]),
        mesh=mesh,
        in_specs=placed,
        out_specs=(P(None, "gx", "gy"), P(None, None, "gx", "gy"), P(None, "gx", "gy")),
        check_vma=False,
    )
```

```python
import functools

import jax
import jax.numpy as jnp
from jax import lax
from jax.experimental import pallas as pl
from jax.experimental.pallas import tpu as pltpu
from jax.sharding import PartitionSpec as P

ITERS = 3
TILE = 128
REACH = 2 * 3 + 1 + ITERS
SEG = 11

gravity = 9.81
time_step = 0.025
MESH = pl.DeviceIdType.MESH


def minmod(a, b):
    return jnp.maximum(jnp.minimum(a, b), 0.0) + jnp.minimum(jnp.maximum(a, b), 0.0)


def hll(left, right, weight, normal):
    hl, hr = left[0], right[0]
    rl, rr = lax.rsqrt(hl), lax.rsqrt(hr)
    ul, ur = left[normal] * (rl * rl), right[normal] * (rr * rr)
    al, ar = gravity**0.5 * (hl * rl), gravity**0.5 * (hr * rr)
    lower = jnp.minimum(jnp.minimum(ul - al, ur - ar), 0.0)
    upper = jnp.maximum(jnp.maximum(ul + al, ur + ar), 0.0)
    scale = weight / (upper - lower)
    low, high = lower * scale, upper * scale
    take_left = high * (ul - lower)
    take_right = low * (upper - ur)
    flux = [take_left * l + take_right * r for l, r in zip(left, right)]
    flux[normal] = flux[normal] + (0.5 * gravity) * (high * hl * hl - low * hr * hr)
    return flux


def lane_next(x):
    return pltpu.roll(x, x.shape[-1] - 1, 1)


def lane_prev(x):
    return pltpu.roll(x, 1, 1)


def kernel(
    nx, ny, rows, cols, layers,
    tile_hbm, depth_hbm, mom_hbm, tracer_hbm, wet_hbm,
    depth_out, mom_out, tracer_out,
    staged, wet_ref, tile_ref, load_sem, pushes,
    fa, fb, fc, wet, pack_l, pack_r, halo_l, halo_r,
    ce, cn, up, inv, z0, z1, z2, part, gather_x, gather_y,
    send_row, recv_row, send_wet, recv_wet, send_col, recv_col,
    send_cor, recv_cor, send_gx, recv_gx, send_gy, recv_gy,
):
    R = REACH
    high_rows = rows + 2 * R
    width = 2 * cols
    half = layers // 2
    gx, gy = lax.axis_index("gx"), lax.axis_index("gy")

    loads = [
        pltpu.make_async_copy(wet_hbm, wet_ref, load_sem.at[0]),
        pltpu.make_async_copy(depth_hbm, staged.at[0], load_sem.at[1]),
        pltpu.make_async_copy(mom_hbm, staged.at[pl.ds(1, 3)], load_sem.at[2]),
        pltpu.make_async_copy(tracer_hbm, staged.at[4], load_sem.at[3]),
        pltpu.make_async_copy(tile_hbm, tile_ref, load_sem.at[4]),
    ]
    for load in loads:
        load.start()

    wet[...] = jnp.zeros_like(wet)
    halo_l[...] = jnp.zeros_like(halo_l)
    halo_r[...] = jnp.zeros_like(halo_r)

    barrier = pltpu.get_barrier_semaphore()
    has = {-1: gx > 0, 1: gx < nx - 1}
    side = {-1: gy > 0, 1: gy < ny - 1}
    for o in range(1, nx):
        pl.semaphore_signal(barrier, inc=1, device_id=(lax.rem(gx + o, nx), gy), device_id_type=MESH)
    for o in range(1, ny):
        pl.semaphore_signal(barrier, inc=1, device_id=(gx, lax.rem(gy + o, ny)), device_id_type=MESH)
    for dx in (-1, 1):
        for dy in (-1, 1):
            @pl.when(jnp.logical_and(has[dx], side[dy]))
            def _(dx=dx, dy=dy):
                pl.semaphore_signal(barrier, inc=1, device_id=(gx + dx, gy + dy), device_id_type=MESH)

    for dx, start in ((-1, 0), (1, R + rows)):
        @pl.when(jnp.logical_not(has[dx]))
        def _(start=start):
            fa[:, start : start + R, :, :cols] = jnp.zeros((5, R, layers, cols), jnp.float32)

    for load in loads:
        load.wait()
    tile = tile_ref[(gx * rows) // TILE, (gy * cols) // TILE].astype(jnp.float32)
    for r in range(rows):
        wet[R + r, :, :cols] = wet_ref[r : r + 1, :].astype(jnp.float32) * tile

    def load_row(r, carry):
        at = pl.ds(r, layers, stride=rows)
        for f in range(5):
            fa[f, R + r, :, :cols] = staged[f, at, :]
        return carry

    lax.fori_loop(0, rows, load_row, 0, unroll=4)

    as_int = lambda flag: flag.astype(jnp.int32)
    corners = (as_int(has[-1]) + as_int(has[1])) * (as_int(side[-1]) + as_int(side[1]))
    pl.semaphore_wait(barrier, nx - 1 + ny - 1 + corners)

    copies = []
    mine = {-1: R, 1: rows}
    theirs = {-1: R + rows, 1: 0}
    pack = {-1: pack_l, 1: pack_r}
    halo = {-1: halo_r, 1: halo_l}
    for i, dx in enumerate((-1, 1)):
        for src, send, recv in ((fa, send_row, recv_row), (wet, send_wet, recv_wet)):
            if src is fa:
                a = fa.at[:, pl.ds(mine[dx], R), :, pl.ds(0, cols)]
                b = fa.at[:, pl.ds(theirs[dx], R), :, pl.ds(0, cols)]
            else:
                a = wet.at[pl.ds(mine[dx], R), :, pl.ds(0, cols)]
                b = wet.at[pl.ds(theirs[dx], R), :, pl.ds(0, cols)]
            send_to = pltpu.make_async_remote_copy(
                src_ref=a, dst_ref=b, send_sem=send.at[i], recv_sem=recv.at[i],
                device_id=(gx + dx, gy), device_id_type=MESH)
            come = pltpu.make_async_remote_copy(
                src_ref=a, dst_ref=b, send_sem=send.at[i], recv_sem=recv.at[1 - i],
                device_id=(gx + dx, gy), device_id_type=MESH)
            copies.append((has[dx], send_to, come))
    for j, dy in enumerate((-1, 1)):
        args = dict(src_ref=pack[dy], dst_ref=halo[dy].at[pl.ds(R, rows)], send_sem=send_col.at[j],
                    device_id=(gx, gy + dy), device_id_type=MESH)
        copies.append((side[dy],
                       pltpu.make_async_remote_copy(recv_sem=recv_col.at[j], **args),
                       pltpu.make_async_remote_copy(recv_sem=recv_col.at[1 - j], **args)))
        for i, dx in enumerate((-1, 1)):
            args = dict(src_ref=pack[dy].at[pl.ds(mine[dx] - R, R)],
                        dst_ref=halo[dy].at[pl.ds(theirs[dx], R)],
                        send_sem=send_cor.at[i, j],
                        device_id=(gx + dx, gy + dy), device_id_type=MESH)
            copies.append((jnp.logical_and(has[dx], side[dy]),
                           pltpu.make_async_remote_copy(recv_sem=recv_cor.at[i, j], **args),
                           pltpu.make_async_remote_copy(recv_sem=recv_cor.at[1 - i, 1 - j], **args)))
    def begin(group):
        for cond, go, come in group:
            @pl.when(cond)
            def _(go=go):
                go.start()

    def finish(group):
        for cond, go, come in group:
            @pl.when(cond)
            def _(go=go, come=come):
                go.wait_send()
                come.wait_recv()

    tall_copies, edge_copies, corner_copies = copies[:4], [copies[4], copies[7]], copies[5:7] + copies[8:]
    begin(tall_copies)

    lane = lax.broadcasted_iota(jnp.int32, (half, cols), 1)

    def pack_row(r, carry):
        left = jnp.zeros((half, cols), jnp.float32)
        right = left
        for s in range(11):
            if s < 10:
                x = fa[s % 5, R + r, (s // 5) * half : (s // 5 + 1) * half, :cols]
            else:
                x = jnp.broadcast_to(wet[R + r, :, :cols], (half, cols))
            mask = jnp.logical_and(lane >= SEG * s, lane < SEG * s + R)
            left = jnp.where(mask, pltpu.roll(x, SEG * s, 1) if s else x, left)
            right = jnp.where(mask, pltpu.roll(x, (SEG * s + R) % cols, 1), right)
        pack_l[r] = left
        pack_r[r] = right
        return carry

    lax.fori_loop(0, rows, pack_row, 0, unroll=4)

    begin(edge_copies)
    begin(corner_copies)
    finish(edge_copies)

    def unpack_row(r, carry):
        fr, fl = halo_r[r], halo_l[r]
        for s in range(11):
            a = pltpu.roll(fr, cols - SEG * s, 1) if s else fr
            b = pltpu.roll(fl, cols - R - SEG * s if SEG * s + R < cols else 2 * cols - R - SEG * s, 1)
            x = jnp.where(lane < R, a, jnp.where(lane >= cols - R, b, 0.0))
            if s < 10:
                fa[s % 5, r, (s // 5) * half : (s // 5 + 1) * half, cols:] = x
            else:
                wet[r, :, cols:] = x[:1]
        return carry

    lax.fori_loop(R, R + rows, unpack_row, 0, unroll=4)

    def transport(src, dst, lo, hi, keep, unroll=4):
        for part_of in range(2):
            cut = slice(part_of * half, (part_of + 1) * half)

            def usable(r):
                w = wet[r]
                u = [src[f, r, cut, :] for f in range(5)]
                u[0] = u[0] * w + (1.0 - w)
                return u

            def sides(u, before, after):
                s = [0.5 * minmod(b, a) for b, a in zip(before, after)]
                return [x - y for x, y in zip(u, s)], [x + y for x, y in zip(u, s)]

            def row_face(i, left):
                here, mid, far = usable(i), usable(i + 1), usable(i + 2)
                right, following = sides(
                    mid, [m - h for m, h in zip(mid, here)], [f - m for f, m in zip(far, mid)])
                return hll(left, right, wet[i] * wet[i + 1], 1), following

            def step(i, carry):
                flux_low, left = carry
                flux_high, following = row_face(i, left)
                u = usable(i)
                d = [lane_next(x) - x for x in u]
                right, left_c = sides(u, [lane_prev(x) for x in d], d)
                w = wet[i]
                across = hll(left_c, [lane_next(x) for x in right], w * lane_next(jnp.broadcast_to(w, (half, width))), 2)
                for f in range(5):
                    rate = -time_step * (flux_high[f] - flux_low[f] + (across[f] - lane_prev(across[f])))
                    old = src[f, i, cut, :]
                    if keep is None:
                        new = old + rate
                    elif keep == 0.75:
                        new = 0.75 * fa[f, i, cut, :] + 0.25 * (old + rate)
                    else:
                        new = fa[f, i, cut, :] * (1.0 / 3.0) + (2.0 / 3.0) * (old + rate)
                    dst[f, i, cut, :] = new
                return flux_high, following

            a, b, c = usable(lo - 2), usable(lo - 1), usable(lo)
            _, left = sides(b, [y - x for x, y in zip(a, b)], [y - x for x, y in zip(b, c)])
            flux, left = row_face(lo - 1, left)
            lax.fori_loop(lo, hi, step, (flux, left), unroll=unroll)

    transport(fa, fb, R + 2, R + rows - 2, None)
    finish(tall_copies)
    finish(corner_copies)
    lax.fori_loop(0, R, unpack_row, 0, unroll=5)
    lax.fori_loop(R + rows, high_rows, unpack_row, 0, unroll=5)
    transport(fa, fb, 2, R + 2, None, 5)
    transport(fa, fb, R + rows - 2, high_rows - 2, None, 5)
    transport(fb, fc, 4, high_rows - 4, 0.75)
    transport(fc, fb, 6, high_rows - 6, 1.0 / 3.0)

    layer_id = lax.broadcasted_iota(jnp.int32, (layers, width), 0)
    top = layer_id == layers - 1

    def above(x):
        return pltpu.roll(x, layers - 1, 0)

    def below(x):
        return pltpu.roll(x, 1, 0)

    def prepare(r, low):
        h, w = fb[0, r], wet[r]
        high = 0.5 * (h + fb[0, r + 1]) * (w * wet[r + 1])
        across = 0.5 * (h + lane_next(h)) * (w * lane_next(jnp.broadcast_to(w, (layers, width))))
        total = jnp.where(top, h, h + above(h))
        upward = jnp.where(jnp.broadcast_to(w, total.shape) > 0.0, 2.0 / total, 0.0)
        inner = jnp.where(top, 0.0, upward)
        diagonal = 0.5 * h + low + high + lane_prev(across) + across + below(inner) + upward
        v = fb[3, r]
        y = fb[2, r]
        div = (
            0.5 * (fb[1, r + 1] - fb[1, r - 1])
            + 0.5 * (lane_next(y) - lane_prev(y))
            + (v - jnp.where(layer_id == 0, 0.0, below(v)))
        )
        force = -div * w
        inverse = jnp.where(diagonal == 0.0, 0.0, 1.0 / diagonal)
        ce[r] = high
        cn[r] = across
        up[r] = upward
        inv[r] = inverse
        z = force * inverse
        z0[r] = z
        return high, force, z

    def fold(x):
        return x[:half, :cols] + x[half:, :cols]

    first = REACH - ITERS
    ce[first - 1] = 0.5 * (fb[0, first - 1] + fb[0, first]) * (wet[first - 1] * wet[first])

    def prep_outer(r, low):
        return prepare(r, low)[0]

    def prep_inner(r, carry):
        low, acc = carry
        high, force, z = prepare(r, low)
        return high, acc + fold(force * z)

    zero = jnp.zeros((half, cols), jnp.float32)
    low = lax.fori_loop(first, R, prep_outer, ce[first - 1], unroll=True)
    low, m0 = lax.fori_loop(R, R + rows, prep_inner, (low, zero), unroll=4)
    lax.fori_loop(R + rows, R + rows + ITERS, prep_outer, low, unroll=True)

    def spread(z, r):
        x = z[r]
        c = cn[r]
        u = jnp.where(top, 0.0, up[r])
        return (
            ce[r - 1] * z[r - 1] + ce[r] * z[r + 1]
            + c * lane_next(x) + lane_prev(c * x)
            + u * above(x) + below(u * x)
        )

    def advance(z, target, reach):
        def outer(r, carry):
            target[r] = spread(z, r) * inv[r]
            return carry

        def inner(r, carry):
            odd, even = carry
            n = spread(z, r)
            y = n * inv[r]
            target[r] = y
            return odd + fold(z[r] * n), even + fold(y * n)

        lax.fori_loop(R - reach, R, outer, 0, unroll=True)
        sums = lax.fori_loop(R, R + rows, inner, (zero, zero), unroll=4)
        lax.fori_loop(R + rows, R + rows + reach, outer, 0, unroll=True)
        return sums

    m1, m2 = advance(z0, z1, 2)
    m3, m4 = advance(z1, z2, 1)
    m5 = lax.fori_loop(R, R + rows, lambda r, acc: acc + fold(z2[r] * spread(z2, r)), zero, unroll=4)

    part[0] = jnp.zeros((8, cols), jnp.float32)
    for k, m in enumerate((m0, m1, m2, m3, m4, m5)):
        part[0, k : k + 1, :] = jnp.sum(m, axis=0, keepdims=True)

    def push_of(k, z):
        def row(r, carry):
            q, c = z[r], cn[r]
            east = 0.5 * (ce[r] * (z[r + 1] - q) + ce[r - 1] * (q - z[r - 1]))
            slope = c * (lane_next(q) - q)
            north = 0.5 * (slope + lane_prev(slope))
            upward = up[r] * (jnp.where(top, 0.0, above(q)) - q)
            for n, push in enumerate((east, north, upward)):
                pushes[k, n, r - R] = push[:, :cols]
            return carry

        lax.fori_loop(R, R + rows, row, 0, unroll=4)

    def everyone(count, slot, gather, send, recv, place):
        moves = [
            pltpu.make_async_remote_copy(
                src_ref=part.at[slot], dst_ref=gather.at[o - 1], send_sem=send.at[o - 1],
                recv_sem=recv.at[o - 1], device_id=place(o), device_id_type=MESH)
            for o in range(1, count)
        ]
        for move in moves:
            move.start()
        return moves

    def plain_out(r, carry):
        at = pl.ds(r - R, layers, stride=rows)
        depth_out[at, :] = fb[0, r, :, :cols]
        tracer_out[at, :] = fb[4, r, :, :cols]
        return carry

    moves = everyone(nx, 0, gather_x, send_gx, recv_gx, lambda o: (lax.rem(gx + o, nx), gy))
    push_of(0, z0)
    push_of(1, z1)
    for move in moves:
        move.wait()
    total = part[0]
    for o in range(nx - 1):
        total = total + gather_x[o]
    part[1] = total
    moves = everyone(ny, 1, gather_y, send_gy, recv_gy, lambda o: (gx, lax.rem(gy + o, ny)))
    push_of(2, z2)
    lax.fori_loop(R, R + rows, plain_out, 0, unroll=4)
    for move in moves:
        move.wait()
    for o in range(ny - 1):
        total = total + gather_y[o]
    sums = jnp.broadcast_to(jnp.sum(total, axis=1, keepdims=True), (8, cols))
    m = [sums[k : k + 1, :] for k in range(6)]

    def dots(a, b, table):
        out = None
        for i in range(3):
            for j in range(3):
                if a[i] is not None and b[j] is not None:
                    t = a[i] * b[j] * table[i + j]
                    out = t if out is None else out + t
        return out

    shifted = [m[k] - m[k + 1] for k in range(5)]

    def plus(a, b, f):
        out = []
        for x, y in zip(a, b):
            out.append(x if y is None else (f * y if x is None else x + f * y))
        return out

    def image(d):
        moved = [None, d[0], d[1]]
        return [x if y is None else (None if x is None and y is None else (-y if x is None else x - y)) for x, y in zip(d, moved)]

    one = jnp.ones_like(m[0])
    direction = [one, None, None]
    residual = [one, None, None]
    pressure = [None, None, None]
    energy = m[0]
    for sweep in range(ITERS):
        bottom = dots(direction, direction, shifted)
        size = energy / bottom
        pressure = plus(pressure, direction, size)
        if sweep + 1 < ITERS:
            residual = plus(residual, image(direction), -size)
            fresh = dots(residual, residual, m)
            direction = plus(residual, direction, fresh / energy)
            energy = fresh

    def correct(r, carry):
        at = pl.ds(r - R, layers, stride=rows)
        for n in range(3):
            push = pressure[0] * pushes[0, n, r - R]
            push = push + pressure[1] * pushes[1, n, r - R] + pressure[2] * pushes[2, n, r - R]
            mom_out[n, at, :] = fb[1 + n, r, :, :cols] - push
        return carry

    lax.fori_loop(R, R + rows, correct, 0, unroll=4)


def body(nx, ny, depth, momentum, tracer, cell_wet, tile_wet):
    layers, rows, cols = depth.shape
    assert TILE % rows == 0 and TILE % cols == 0 and cols == 128 and rows >= REACH
    f32 = jnp.float32
    tall = rows + 2 * REACH
    wide = 2 * cols
    half = layers // 2
    dma = pltpu.SemaphoreType.DMA
    vmem = pl.BlockSpec(memory_space=pltpu.VMEM)
    flat = jax.ShapeDtypeStruct((layers * rows, cols), f32)
    field = pltpu.VMEM((5, tall, layers, wide), f32)
    layer = pltpu.VMEM((tall, layers, wide), f32)
    packed = pltpu.VMEM((rows, half, cols), f32)
    halo = pltpu.VMEM((tall, half, cols), f32)
    pairs = [dma((2,))] * 6 + [dma((2, 2))] * 2 + [dma((nx - 1,))] * 2 + [dma((ny - 1,))] * 2
    new_depth, new_momentum, new_tracer = pl.pallas_call(
        functools.partial(kernel, nx, ny, rows, cols, layers),
        out_shape=(flat, jax.ShapeDtypeStruct((3, layers * rows, cols), f32), flat),
        in_specs=[pl.BlockSpec(memory_space=pltpu.HBM)] * 5,
        out_specs=(vmem, vmem, vmem),
        scratch_shapes=[
            pltpu.VMEM((5, layers * rows, cols), f32),
            pltpu.VMEM((rows, cols), jnp.int32),
            pltpu.SMEM(tile_wet.shape, jnp.int32),
            dma((5,)),
            pltpu.VMEM((3, 3, rows, layers, cols), f32),
            field, field, field,
            pltpu.VMEM((tall, 1, wide), f32),
            packed, packed, halo, halo,
            layer, layer, layer, layer, layer, layer, layer,
            pltpu.VMEM((2, 8, cols), f32),
            pltpu.VMEM((nx - 1, 8, cols), f32),
            pltpu.VMEM((ny - 1, 8, cols), f32),
            *pairs,
        ],
        compiler_params=pltpu.CompilerParams(
            collective_id=0, has_side_effects=True, vmem_limit_bytes=56 * 1024 * 1024
        ),
    )(
        tile_wet,
        depth.reshape(layers * rows, cols),
        momentum.reshape(3, layers * rows, cols),
        tracer.reshape(layers * rows, cols),
        cell_wet,
    )
    return (
        new_depth.reshape(depth.shape),
        new_momentum.reshape(momentum.shape),
        new_tracer.reshape(tracer.shape),
    )


def solution(mesh):
    placed = (
        P(None, "gx", "gy"),
        P(None, None, "gx", "gy"),
        P(None, "gx", "gy"),
        P("gx", "gy"),
        P(),
    )
    return jax.shard_map(
        functools.partial(body, mesh.shape["gx"], mesh.shape["gy"]),
        mesh=mesh,
        in_specs=placed,
        out_specs=(P(None, "gx", "gy"), P(None, None, "gx", "gy"), P(None, "gx", "gy")),
        check_vma=False,
    )
```
